128 devices in a mesh: chan: 16 (over x, y_lo, core), win: 8 (over y_hi, z).
Axes of the slice: x: 4, y: 4 (y_hi: 2, y_lo: 2; y = y_hi * 2 + y_lo), z: 4, core: 2. Of those that a mesh axis runs over, the one named last changes fastest.
Arguments:
- traces: bfloat16 [128, 1024, 512], P('win', 'chan'), may hold values from -80 to 80
- valid: int32 [128, 1024], P('win', 'chan'), may hold values 0 or 1
- reach: int32 [1024], P('chan'), may hold values from 1 to 256
Outputs:
- stack: float32 [256, 1024, 256], P('win', 'chan')
The draws below stay inside these ranges and needn't reach their ends.
All inputs are finite; a program needn't handle non-finite values. No bound on the sum of `valid` on one device may be relied on, other than what follows from the above.
Results may differ from the reference program's by a relative error of at most 0.0045.
Values may be sent and summed in bfloat16 or wider, within the bound.
A program may use at most 128 MiB of HBM per device.

```python
import math
import jax
import jax.numpy as jnp
from jax import lax

S = 512
F = 128
FIRST = 16
BAND = 256
CHANNELS = 1024
WINDOWS = 128


def draw_traces(key, part):
    key_noise = jax.random.fold_in(key, 11)
    key_scale = jax.random.fold_in(key, 12)
    noise = jnp.clip(jax.random.normal(key_noise, (WINDOWS, CHANNELS, S), jnp.float32), -6.0, 6.0)
    scales = jnp.exp(jax.random.uniform(key_scale, (WINDOWS, CHANNELS, 1), jnp.float32, 0.0, jnp.log(10.0)))
    return (noise * scales).astype(jnp.bfloat16)


def set_ends(result, rng, low, top_value):
    longest = result.shape.index(max(result.shape))
    spots = []
    for shift in (0, 1):
        where = [jax.random.randint(jax.random.fold_in(rng, axis), (), 0, length) for axis, length in enumerate(result.shape)]
        where[longest] = (where[longest] + shift) % result.shape[longest]
        spots.append(tuple(where))
    return result.at[spots[0]].set(low).at[spots[1]].set(top_value)


def setup_inputs(seed: int = 0) -> dict:
    splits = jax.random.split(jax.random.key(seed), 4)
    return {
        "traces": draw_traces(jax.random.fold_in(splits[3], 71), 0),
        "valid": set_ends((jax.random.randint(splits[1], (WINDOWS, CHANNELS), 0, 8) < 7).astype(jnp.int32), jax.random.fold_in(splits[1], 1), 0, 1),
        "reach": set_ends(jax.random.randint(splits[2], (CHANNELS,), 1, BAND + 1), jax.random.fold_in(splits[2], 1), 1, BAND).astype(jnp.int32),
    }


def make_table():
    t_int = jnp.arange(S, dtype=jnp.int32)
    j_int = jnp.arange(F, dtype=jnp.int32) + FIRST
    phase = t_int[:, None] * j_int[None, :] % S
    angle = 2.0 * math.pi / S * phase.astype(jnp.float32)
    hann = 0.5 - 0.5 * jnp.cos(2.0 * math.pi / S * t_int.astype(jnp.float32))
    return jnp.concatenate([hann[:, None] * jnp.cos(angle), -hann[:, None] * jnp.sin(angle)], axis=1).astype(jnp.bfloat16)

def whiten(spectra, valid):
    real_part = spectra[..., :F]
    imag_part = spectra[..., F:]
    amplitude = jnp.sqrt(real_part * real_part + imag_part * imag_part)
    level = jnp.sqrt(lax.optimization_barrier(jnp.mean(amplitude * amplitude, axis=-1, keepdims=True)) + 1e-06)
    factor = valid.astype(jnp.float32)[..., None] / (amplitude + 0.1 * level)
    return jnp.concatenate([real_part * factor, imag_part * factor], axis=-1).astype(jnp.bfloat16)

def reference(traces, valid, reach):
    table = make_table()
    spectra = jnp.einsum('wct,tj->wcj', traces, table, preferred_element_type=jnp.float32)
    whitened = whiten(spectra, valid).astype(jnp.float32)
    scale = 1.0 / math.sqrt(WINDOWS)
    a_re = whitened[..., :F]
    a_im = whitened[..., F:]

    def one_offset(offset):
        rolled = jnp.roll(whitened, -offset, axis=1)
        b_re = rolled[..., :F]
        b_im = rolled[..., F:]
        real_sum = lax.optimization_barrier(jnp.sum(a_re * b_re + a_im * b_im, axis=0))
        imag_sum = lax.optimization_barrier(jnp.sum(a_im * b_re - a_re * b_im, axis=0))
        inside = (offset < reach).astype(jnp.float32)
        return jnp.concatenate([real_sum, imag_sum], axis=-1) * inside[:, None] * scale
    return lax.map(one_offset, jnp.arange(BAND, dtype=jnp.int32))
```

```python
import functools
import math

import jax
import jax.numpy as jnp
import numpy as np
from jax import lax
from jax.experimental import pallas as pl
from jax.experimental.pallas import tpu as pltpu
from jax.sharding import PartitionSpec as P

F = 128
FIRST = 16
BAND = 256
LANES = 128
MESH = pl.DeviceIdType.MESH


def table_rows(samples):
    t_int = np.arange(samples, dtype=np.int64)
    j_int = np.arange(F, dtype=np.int64) + FIRST
    angle = 2.0 * np.pi / samples * (j_int[:, None] * t_int[None, :] % samples)
    hann = 0.5 - 0.5 * np.cos(2.0 * np.pi / samples * t_int)
    rows = np.concatenate([hann * np.cos(angle), -hann * np.sin(angle)], axis=0)
    return rows.astype(np.float32).astype(jnp.bfloat16)


def exchange_kernel(
    groups, near, table_ref, traces_ref, valid_ref, out_ref,
    spread, mine, every, rows, cols, stack,
    send_in, recv_in, send_halo, recv_halo, send_out, recv_out, local_sem,
):
    chan = lax.axis_index("chan")
    win = lax.axis_index("win")
    ring = lax.axis_size("chan")
    lane_of = chan % near
    base = chan - lane_of
    team = near * groups
    bins = F // team
    me = lane_of * groups + win
    width = traces_ref.shape[1]
    local = traces_ref.shape[0]
    ahead = lax.rem(chan + near, ring)
    behind = lax.rem(chan + ring - near, ring)

    def device_of(t):
        return {"chan": base + t // groups, "win": lax.rem(t, groups)}

    barrier = pltpu.get_barrier_semaphore()

    def greet(step, carry):
        pl.semaphore_signal(
            barrier, inc=1, device_id=device_of(lax.rem(me + step, team)), device_id_type=MESH
        )
        return carry

    lax.fori_loop(1, team, greet, 0)
    for other in (ahead, behind):
        pl.semaphore_signal(
            barrier, inc=1, device_id={"chan": other, "win": win}, device_id_type=MESH
        )

    lane = lax.broadcasted_iota(jnp.int32, (1, LANES), 1)
    first_half = lane < width
    valid_twice = jnp.concatenate([valid_ref[...], valid_ref[...]], axis=1).astype(jnp.float32)
    table = table_ref[...]
    for pair in range(local // 2):
        samples = traces_ref[2 * pair : 2 * pair + 2].reshape(2 * width, traces_ref.shape[2])
        spectra = lax.dot_general(
            table, samples, (((1,), (1,)), ((), ())), preferred_element_type=jnp.float32
        )
        re = spectra[:F]
        im = spectra[F:]
        power = re * re + im * im
        amplitude = jnp.sqrt(power)
        level = jnp.sqrt(jnp.mean(power, axis=0, keepdims=True) + 1e-06)
        usable = jnp.where(
            first_half, valid_twice[2 * pair : 2 * pair + 1], valid_twice[2 * pair + 1 : 2 * pair + 2]
        )
        factor = usable / (amplitude + 0.1 * level)
        re = re * factor
        im = im * factor
        spread[2 * pair * F : (2 * pair + 1) * F, :] = jnp.where(
            first_half, re, pltpu.roll(im, width, 1)
        )
        spread[(2 * pair + 1) * F : (2 * pair + 2) * F, :] = jnp.where(
            first_half, pltpu.roll(re, width, 1), im
        )

    def gather_bin(index, carry):
        mine[index] = spread[pl.ds(index, local, stride=F), :].astype(jnp.bfloat16)
        return carry

    lax.fori_loop(0, F, gather_bin, 0, unroll=8)

    pl.semaphore_wait(barrier, team + 1)

    def send_bins(step, carry):
        t = lax.rem(me + step, team)
        pltpu.make_async_remote_copy(
            src_ref=mine.at[pl.ds(t * bins, bins)],
            dst_ref=every.at[me],
            send_sem=send_in,
            recv_sem=recv_in,
            device_id=device_of(t),
            device_id_type=MESH,
        ).start()
        return carry

    lax.fori_loop(1, team, send_bins, 0)
    every[me] = mine[pl.ds(me * bins, bins)]
    arrived = every.at[pl.ds(0, team - 1)]
    pltpu.make_async_copy(arrived, arrived, recv_in).wait()

    own = near * width
    for b in range(bins):
        for a in range(near):
            block = every[groups * a : groups * (a + 1), b].reshape(groups * local, LANES)
            wide = block.astype(jnp.float32)
            turned = wide.T.astype(jnp.bfloat16)
            rows[b, width * a : width * (a + 1), :F] = turned[:width]
            rows[b, width * a : width * (a + 1), F:] = turned[width:]
            swapped = pltpu.roll(wide, width, 1)
            cols[b, a, :F] = block
            cols[b, a, F:] = jnp.where(first_half, swapped, -swapped).astype(jnp.bfloat16)
        pltpu.make_async_remote_copy(
            src_ref=rows.at[b, pl.ds(0, own)],
            dst_ref=rows.at[b, pl.ds(own, own)],
            send_sem=send_halo.at[b],
            recv_sem=recv_halo.at[b],
            device_id={"chan": behind, "win": win},
            device_id_type=MESH,
        ).start()

    shift = lax.rem(lax.broadcasted_iota(jnp.int32, (1, LANES), 1), width)
    band = BAND // groups
    for b in range(bins):
        halo = rows.at[b, pl.ds(own, own)]
        pltpu.make_async_copy(halo, halo, recv_halo.at[b]).wait()
        for a in range(near):
            product = jnp.dot(
                rows[b, width * a : width * a + width + BAND],
                cols[b, a],
                preferred_element_type=jnp.float32,
            )
            by = width // 2
            while by >= 8:
                product = jnp.where((shift & by) != 0, product[by:], product[:-by])
                by //= 2
            size = product.shape[0]
            while by >= 1:
                product = jnp.where((shift & by) != 0, pltpu.roll(product, size - by, 0), product)
                by //= 2
            stack[b, a] = product[:BAND].astype(jnp.bfloat16)

        def send_stack(step, carry):
            t = lax.rem(me + step, team)
            pltpu.make_async_remote_copy(
                src_ref=stack.at[b, t // groups, pl.ds(lax.rem(t, groups) * band, band)],
                dst_ref=out_ref.at[me * bins + b],
                send_sem=send_out,
                recv_sem=recv_out,
                device_id=device_of(t),
                device_id_type=MESH,
            ).start()
            return carry

        lax.fori_loop(1, team, send_stack, 0)
        pltpu.make_async_copy(
            stack.at[b, lane_of, pl.ds(win * band, band)], out_ref.at[me * bins + b], local_sem.at[b]
        ).start()

    for b in range(bins):
        pltpu.make_async_copy(
            stack.at[b, lane_of, pl.ds(win * band, band)], out_ref.at[me * bins + b], local_sem.at[b]
        ).wait()
        halo = rows.at[b, pl.ds(0, own)]
        pltpu.make_async_copy(halo, halo, send_halo.at[b]).wait()
    pltpu.make_async_copy(arrived, arrived, send_in).wait()
    landed = out_ref.at[pl.ds(0, (team - 1) * bins)]
    pltpu.make_async_copy(landed, landed, send_out).wait()
    pltpu.make_async_copy(landed, landed, recv_out).wait()


def exchange(traces, valid, groups, near):
    local, width, samples = traces.shape
    team = near * groups
    bins = F // team
    own = near * width
    bf16 = jnp.bfloat16
    return pl.pallas_call(
        functools.partial(exchange_kernel, groups, near),
        out_shape=jax.ShapeDtypeStruct((F, BAND // groups, LANES), bf16),
        in_specs=[pl.BlockSpec(memory_space=pltpu.VMEM)] * 3,
        out_specs=pl.BlockSpec(memory_space=pl.ANY),
        scratch_shapes=[
            pltpu.VMEM((local * F, LANES), jnp.float32),
            pltpu.VMEM((F, local, LANES), bf16),
            pltpu.VMEM((team, bins, local, LANES), bf16),
            pltpu.VMEM((bins, 2 * own, 2 * F), bf16),
            pltpu.VMEM((bins, near, 2 * F, LANES), bf16),
            pltpu.VMEM((bins, near, BAND, LANES), bf16),
            pltpu.SemaphoreType.DMA,
            pltpu.SemaphoreType.DMA,
            pltpu.SemaphoreType.DMA((bins,)),
            pltpu.SemaphoreType.DMA((bins,)),
            pltpu.SemaphoreType.DMA,
            pltpu.SemaphoreType.DMA,
            pltpu.SemaphoreType.DMA((bins,)),
        ],
        compiler_params=pltpu.CompilerParams(collective_id=0, has_side_effects=True),
        name="exchange",
    )(table_rows(samples), traces, valid)


def finish_kernel(scale, steps, stack_ref, reach_ref, out_ref, wide):
    offsets = out_ref.shape[0]
    width = out_ref.shape[1]
    wide[...] = stack_ref[...].astype(jnp.float32).reshape(F * offsets, LANES)
    reach = jnp.concatenate([reach_ref[...], reach_ref[...]], axis=1)
    first = (lax.axis_index("win") * steps + pl.program_id(0)) * offsets

    def one(k, carry):
        piece = wide[pl.ds(k, F, stride=offsets), :]
        turned = (piece * jnp.where(first + k < reach, scale, 0.0)).T
        out_ref[k, :, :F] = turned[:width]
        out_ref[k, :, F:] = turned[width:]
        return carry

    lax.fori_loop(0, offsets, one, 0, unroll=2)


def finish(stacked, reach, windows):
    band = stacked.shape[1]
    width = reach.shape[0]
    steps = 2
    offsets = band // steps
    return pl.pallas_call(
        functools.partial(finish_kernel, 1.0 / math.sqrt(windows), steps),
        out_shape=jax.ShapeDtypeStruct((band, width, 2 * F), jnp.float32),
        grid=(steps,),
        in_specs=[
            pl.BlockSpec((F, offsets, LANES), lambda s: (0, s, 0)),
            pl.BlockSpec((1, width), lambda s: (0, 0)),
        ],
        out_specs=pl.BlockSpec((offsets, width, 2 * F), lambda s: (s, 0, 0)),
        scratch_shapes=[pltpu.VMEM((F * offsets, LANES), jnp.float32)],
        name="finish",
    )(stacked, reach.reshape(1, width))


def on_device(groups, near, traces, valid, reach):
    stacked = exchange(traces, valid, groups, near)
    return finish(stacked, reach, traces.shape[0] * groups)


def solution(mesh):
    groups = mesh.shape["win"]
    near = BAND // (1024 // mesh.shape["chan"])
    in_specs = (P("win", "chan", None), P("win", "chan"), P("chan"))
    return jax.shard_map(
        functools.partial(on_device, groups, near),
        mesh=mesh,
        in_specs=in_specs,
        out_specs=P("win", "chan", None),
        check_vma=False,
    )
```

```python
import functools
import math

import jax
import jax.numpy as jnp
import numpy as np
from jax import lax
from jax.experimental import pallas as pl
from jax.experimental.pallas import tpu as pltpu
from jax.sharding import PartitionSpec as P

F = 128
FIRST = 16
BAND = 256
LANES = 128
MESH = pl.DeviceIdType.MESH


def table_rows(samples):
    t_int = np.arange(samples, dtype=np.int64)
    j_int = np.arange(F, dtype=np.int64) + FIRST
    angle = 2.0 * np.pi / samples * (j_int[:, None] * t_int[None, :] % samples)
    hann = 0.5 - 0.5 * np.cos(2.0 * np.pi / samples * t_int)
    rows = np.concatenate([hann * np.cos(angle), -hann * np.sin(angle)], axis=0)
    return rows.astype(np.float32).astype(jnp.bfloat16)


def exchange_kernel(
    groups, near, table_ref, traces_ref, valid_ref, out_ref,
    spread, mine, every, rows, cols, stack,
    send_in, recv_in, send_halo, recv_halo, send_out, recv_out, local_sem,
):
    chan = lax.axis_index("chan")
    win = lax.axis_index("win")
    ring = lax.axis_size("chan")
    depth = groups // 2
    cores = near // 2
    lane_of = lax.rem(chan, near)
    base = chan - lane_of
    team = near * groups
    bins = F // team
    me = lane_of * groups + win
    width = traces_ref.shape[1]
    local = traces_ref.shape[0]
    ahead = lax.rem(chan + near, ring)
    behind = lax.rem(chan + ring - near, ring)

    y_hi, z = win // depth, lax.rem(win, depth)
    y_lo, core = lane_of // cores, lax.rem(lane_of, cores)

    def hops(step):
        d_hi, d_lo, d_z, d_core = step
        return (1 if d_lo else 2 * d_hi) + min(d_z, depth - d_z)

    steps = [
        (d_hi, d_lo, d_z, d_core)
        for d_hi in range(2)
        for d_lo in range(2)
        for d_z in range(depth)
        for d_core in range(cores)
    ]
    steps.sort(key=lambda step: (-hops(step), step))
    steps.remove((0, 0, 0, 0))

    def win_at(d_hi, d_z):
        return lax.rem(y_hi + d_hi, 2) * depth + lax.rem(z + d_z, depth)

    def lane_at(d_lo, d_core):
        return lax.rem(y_lo + d_lo, 2) * cores + lax.rem(core + d_core, cores)

    barrier = pltpu.get_barrier_semaphore()
    for d_hi, d_lo, d_z, d_core in steps:
        pl.semaphore_signal(
            barrier,
            inc=1,
            device_id={"chan": base + lane_at(d_lo, d_core), "win": win_at(d_hi, d_z)},
            device_id_type=MESH,
        )
    for other in (ahead, behind):
        pl.semaphore_signal(
            barrier, inc=1, device_id={"chan": other, "win": win}, device_id_type=MESH
        )

    lane = lax.broadcasted_iota(jnp.int32, (1, LANES), 1)
    first_half = lane < width
    valid_twice = jnp.concatenate([valid_ref[...], valid_ref[...]], axis=1).astype(jnp.float32)
    table = table_ref[...]
    for pair in range(local // 2):
        samples = traces_ref[2 * pair : 2 * pair + 2].reshape(2 * width, traces_ref.shape[2])
        spectra = lax.dot_general(
            table, samples, (((1,), (1,)), ((), ())), preferred_element_type=jnp.float32
        )
        re = spectra[:F]
        im = spectra[F:]
        power = re * re + im * im
        amplitude = jnp.sqrt(power)
        level = jnp.sqrt(jnp.mean(power, axis=0, keepdims=True) + 1e-06)
        usable = jnp.where(
            first_half, valid_twice[2 * pair : 2 * pair + 1], valid_twice[2 * pair + 1 : 2 * pair + 2]
        )
        factor = usable / (amplitude + 0.1 * level)
        re = re * factor
        im = im * factor
        spread[2 * pair * F : (2 * pair + 1) * F, :] = jnp.where(
            first_half, re, pltpu.roll(im, width, 1)
        )
        spread[(2 * pair + 1) * F : (2 * pair + 2) * F, :] = jnp.where(
            first_half, pltpu.roll(re, width, 1), im
        )

    def gather_bins(b):
        def gather_bin(t, carry):
            index = b * team + t
            mine[index] = spread[pl.ds(index, local, stride=F), :].astype(jnp.bfloat16)
            return carry

        lax.fori_loop(0, team, gather_bin, 0, unroll=8)

    gather_bins(0)
    pl.semaphore_wait(barrier, team + 1)

    def send_bins(b, carry):
        for d_hi, d_lo, d_z, d_core in steps:
            to_lane, to_win = lane_at(d_lo, d_core), win_at(d_hi, d_z)
            pltpu.make_async_remote_copy(
                src_ref=mine.at[b * team + to_lane * groups + to_win],
                dst_ref=every.at[b, me],
                send_sem=send_in,
                recv_sem=recv_in.at[b],
                device_id={"chan": base + to_lane, "win": to_win},
                device_id_type=MESH,
            ).start()
        every[b, me] = mine[b * team + me]

        @pl.when(b + 1 < bins)
        def _():
            gather_bins(b + 1)

        return carry

    lax.fori_loop(0, bins, send_bins, 0)

    own = near * width
    for b in range(bins):
        arrived = every.at[b, pl.ds(0, team - 1)]
        pltpu.make_async_copy(arrived, arrived, recv_in.at[b]).wait()
        for a in range(near):
            block = every[b, groups * a : groups * (a + 1)].reshape(groups * local, LANES)
            wide = block.astype(jnp.float32)
            turned = wide.T.astype(jnp.bfloat16)
            rows[b, width * a : width * (a + 1), :F] = turned[:width]
            rows[b, width * a : width * (a + 1), F:] = turned[width:]
            swapped = pltpu.roll(wide, width, 1)
            cols[b, a, :F] = block
            cols[b, a, F:] = jnp.where(first_half, swapped, -swapped).astype(jnp.bfloat16)
        for a in range(near):
            pltpu.make_async_remote_copy(
                src_ref=rows.at[b, pl.ds(width * a, width)],
                dst_ref=rows.at[b, pl.ds(own + width * a, width)],
                send_sem=send_halo,
                recv_sem=recv_halo.at[b * near + a],
                device_id={"chan": behind, "win": win},
                device_id_type=MESH,
            ).start()

    shift = lax.rem(lax.broadcasted_iota(jnp.int32, (1, LANES), 1), width)
    band = BAND // groups
    order = sorted({(step[0], step[2]) for step in steps}, key=lambda s: -hops((s[0], 0, s[1], 0)))
    for b in range(bins):
        for a in range(near):
            halo = rows.at[b, pl.ds(own + width * a, width)]
            pltpu.make_async_copy(halo, halo, recv_halo.at[b * near + a]).wait()
            product = jnp.dot(
                rows[b, width * a : width * a + width + BAND],
                cols[b, a],
                preferred_element_type=jnp.float32,
            )
            by = width // 2
            while by >= 8:
                product = jnp.where((shift & by) != 0, product[by:], product[:-by])
                by //= 2
            size = product.shape[0]
            while by >= 1:
                product = jnp.where((shift & by) != 0, pltpu.roll(product, size - by, 0), product)
                by //= 2
            stack[b, a] = product[:BAND].astype(jnp.bfloat16)

            def send_stack(d_hi, d_z, b=b, a=a):
                to_win = win_at(d_hi, d_z)
                pltpu.make_async_remote_copy(
                    src_ref=stack.at[b, a, pl.ds(to_win * band, band)],
                    dst_ref=out_ref.at[b * team + me],
                    send_sem=send_out,
                    recv_sem=recv_out,
                    device_id={"chan": base + a, "win": to_win},
                    device_id_type=MESH,
                ).start()

            for d_hi, d_z in order[:-1]:
                send_stack(d_hi, d_z)

            @pl.when(lane_of != a)
            def _(b=b, a=a):
                send_stack(0, 0)

            @pl.when(lane_of == a)
            def _(b=b, a=a):
                pltpu.make_async_copy(
                    stack.at[b, a, pl.ds(win * band, band)], out_ref.at[b * team + me], local_sem
                ).start()

    sent = mine.at[pl.ds(0, bins * (team - 1))]
    pltpu.make_async_copy(sent, sent, send_in).wait()
    halo = rows.at[pl.ds(0, bins), pl.ds(0, own)]
    pltpu.make_async_copy(halo, halo, send_halo).wait()
    here = out_ref.at[pl.ds(0, bins)]
    pltpu.make_async_copy(here, here, local_sem).wait()
    landed = out_ref.at[pl.ds(0, (team - 1) * bins)]
    pltpu.make_async_copy(landed, landed, send_out).wait()
    pltpu.make_async_copy(landed, landed, recv_out).wait()


def exchange(traces, valid, groups, near):
    local, width, samples = traces.shape
    team = near * groups
    bins = F // team
    own = near * width
    bf16 = jnp.bfloat16
    return pl.pallas_call(
        functools.partial(exchange_kernel, groups, near),
        out_shape=jax.ShapeDtypeStruct((F, BAND // groups, LANES), bf16),
        in_specs=[pl.BlockSpec(memory_space=pltpu.VMEM)] * 3,
        out_specs=pl.BlockSpec(memory_space=pl.ANY),
        scratch_shapes=[
            pltpu.VMEM((local * F, LANES), jnp.float32),
            pltpu.VMEM((F, local, LANES), bf16),
            pltpu.VMEM((bins, team, local, LANES), bf16),
            pltpu.VMEM((bins, 2 * own, 2 * F), bf16),
            pltpu.VMEM((bins, near, 2 * F, LANES), bf16),
            pltpu.VMEM((bins, near, BAND, LANES), bf16),
            pltpu.SemaphoreType.DMA,
            pltpu.SemaphoreType.DMA((bins,)),
            pltpu.SemaphoreType.DMA,
            pltpu.SemaphoreType.DMA((bins * near,)),
            pltpu.SemaphoreType.DMA,
            pltpu.SemaphoreType.DMA,
            pltpu.SemaphoreType.DMA,
        ],
        compiler_params=pltpu.CompilerParams(collective_id=0, has_side_effects=True),
        name="exchange",
    )(table_rows(samples), traces, valid)


def finish_kernel(scale, steps, stack_ref, reach_ref, out_ref, wide):
    offsets = out_ref.shape[0]
    width = out_ref.shape[1]
    wide[...] = stack_ref[...].astype(jnp.float32).reshape(F * offsets, LANES)
    reach = jnp.concatenate([reach_ref[...], reach_ref[...]], axis=1)
    first = (lax.axis_index("win") * steps + pl.program_id(0)) * offsets

    def one(k, carry):
        piece = wide[pl.ds(k, F, stride=offsets), :]
        turned = (piece * jnp.where(first + k < reach, scale, 0.0)).T
        out_ref[k, :, :F] = turned[:width]
        out_ref[k, :, F:] = turned[width:]
        return carry

    lax.fori_loop(0, offsets, one, 0, unroll=2)


def finish(stacked, reach, windows):
    band = stacked.shape[1]
    width = reach.shape[0]
    steps = 2
    offsets = band // steps
    return pl.pallas_call(
        functools.partial(finish_kernel, 1.0 / math.sqrt(windows), steps),
        out_shape=jax.ShapeDtypeStruct((band, width, 2 * F), jnp.float32),
        grid=(steps,),
        in_specs=[
            pl.BlockSpec((F, offsets, LANES), lambda s: (0, s, 0)),
            pl.BlockSpec((1, width), lambda s: (0, 0)),
        ],
        out_specs=pl.BlockSpec((offsets, width, 2 * F), lambda s: (s, 0, 0)),
        scratch_shapes=[pltpu.VMEM((F * offsets, LANES), jnp.float32)],
        name="finish",
    )(stacked, reach.reshape(1, width))


def on_device(groups, near, traces, valid, reach):
    stacked = exchange(traces, valid, groups, near)
    return finish(stacked, reach, traces.shape[0] * groups)


def solution(mesh):
    groups = mesh.shape["win"]
    near = BAND // (1024 // mesh.shape["chan"])
    in_specs = (P("win", "chan", None), P("win", "chan"), P("chan"))
    return jax.shard_map(
        functools.partial(on_device, groups, near),
        mesh=mesh,
        in_specs=in_specs,
        out_specs=P("win", "chan", None),
        check_vma=False,
    )
```

```python
import functools
import math

import jax
import jax.numpy as jnp
import numpy as np
from jax import lax
from jax.experimental import pallas as pl
from jax.experimental.pallas import tpu as pltpu
from jax.sharding import PartitionSpec as P

F = 128
FIRST = 16
BAND = 256
LANES = 128
MESH = pl.DeviceIdType.MESH


def table_rows(samples):
    t_int = np.arange(samples, dtype=np.int64)
    j_int = np.arange(F, dtype=np.int64) + FIRST
    angle = 2.0 * np.pi / samples * (j_int[:, None] * t_int[None, :] % samples)
    hann = 0.5 - 0.5 * np.cos(2.0 * np.pi / samples * t_int)
    rows = np.concatenate([hann * np.cos(angle), -hann * np.sin(angle)], axis=0)
    return rows.astype(np.float32).astype(jnp.bfloat16)


def exchange_kernel(
    groups, near, scale, table_hbm, traces_hbm, valid_hbm, reach_hbm, out_ref, weight_ref,
    table_ref, traces_ref, valid_ref, reach_ref, spread, mine, every, rows, cols, stack, landing, wide,
    load_sem, send_in, recv_in, send_halo, recv_halo, send_out, recv_out,
):
    chan = lax.axis_index("chan")
    win = lax.axis_index("win")
    ring = lax.axis_size("chan")
    depth = groups // 2
    cores = near // 2
    lane_of = lax.rem(chan, near)
    base = chan - lane_of
    team = near * groups
    bins = F // team
    me = lane_of * groups + win
    width = traces_ref.shape[1]
    local = traces_ref.shape[0]
    ahead = lax.rem(chan + near, ring)
    behind = lax.rem(chan + ring - near, ring)

    y_hi, z = win // depth, lax.rem(win, depth)
    y_lo, core = lane_of // cores, lax.rem(lane_of, cores)

    def hops(step):
        d_hi, d_lo, d_z, d_core = step
        return (1 if d_lo else 2 * d_hi) + min(d_z, depth - d_z)

    steps = [
        (d_hi, d_lo, d_z, d_core)
        for d_hi in range(2)
        for d_lo in range(2)
        for d_z in range(depth)
        for d_core in range(cores)
    ]
    steps.sort(key=lambda step: (-hops(step), step))
    steps.remove((0, 0, 0, 0))

    def win_at(d_hi, d_z):
        return lax.rem(y_hi + d_hi, 2) * depth + lax.rem(z + d_z, depth)

    def lane_at(d_lo, d_core):
        return lax.rem(y_lo + d_lo, 2) * cores + lax.rem(core + d_core, cores)

    loads = [
        pltpu.make_async_copy(table_hbm, table_ref, load_sem.at[0]),
        pltpu.make_async_copy(traces_hbm, traces_ref, load_sem.at[1]),
        pltpu.make_async_copy(valid_hbm, valid_ref, load_sem.at[2]),
        pltpu.make_async_copy(reach_hbm, reach_ref, load_sem.at[3]),
    ]
    for load in loads:
        load.start()

    barrier = pltpu.get_barrier_semaphore()
    for d_hi, d_lo, d_z, d_core in steps:
        pl.semaphore_signal(
            barrier,
            inc=1,
            device_id={"chan": base + lane_at(d_lo, d_core), "win": win_at(d_hi, d_z)},
            device_id_type=MESH,
        )
    for other in (ahead, behind):
        pl.semaphore_signal(
            barrier, inc=1, device_id={"chan": other, "win": win}, device_id_type=MESH
        )

    for load in loads:
        load.wait()

    lane = lax.broadcasted_iota(jnp.int32, (1, LANES), 1)
    first_half = lane < width
    valid_twice = jnp.concatenate([valid_ref[...], valid_ref[...]], axis=1).astype(jnp.float32)
    for pair in range(local // 2):
        samples = traces_ref[2 * pair : 2 * pair + 2].reshape(2 * width, traces_ref.shape[2])
        spectra = lax.dot_general(
            table_ref[...], samples, (((1,), (1,)), ((), ())), preferred_element_type=jnp.float32
        )
        re = spectra[:F]
        im = spectra[F:]
        power = re * re + im * im
        amplitude = jnp.sqrt(power)
        level = jnp.sqrt(jnp.mean(power, axis=0, keepdims=True) + 1e-06)
        usable = jnp.where(
            first_half, valid_twice[2 * pair : 2 * pair + 1], valid_twice[2 * pair + 1 : 2 * pair + 2]
        )
        factor = usable / (amplitude + 0.1 * level)
        re = re * factor
        im = im * factor
        spread[2 * pair * F : 2 * pair * F + F, :] = jnp.where(
            first_half, re, pltpu.roll(im, width, 1)
        )
        spread[(2 * pair + 1) * F : (2 * pair + 1) * F + F, :] = jnp.where(
            first_half, pltpu.roll(re, width, 1), im
        )

    def gather_bin(index, carry):
        mine[index] = spread[pl.ds(index, local, stride=F), :].astype(jnp.bfloat16)
        return carry

    lax.fori_loop(0, F, gather_bin, 0, unroll=8)
    pl.semaphore_wait(barrier, team + 1)

    def send_bins(b, carry):
        for d_hi, d_lo, d_z, d_core in steps:
            to_lane, to_win = lane_at(d_lo, d_core), win_at(d_hi, d_z)
            pltpu.make_async_remote_copy(
                src_ref=mine.at[b * team + to_lane * groups + to_win],
                dst_ref=every.at[b, me],
                send_sem=send_in,
                recv_sem=recv_in.at[b],
                device_id={"chan": base + to_lane, "win": to_win},
                device_id_type=MESH,
            ).start()
        every[b, me] = mine[b * team + me]
        return carry

    lax.fori_loop(0, bins, send_bins, 0)

    own = near * width

    def turn(b):
        arrived = every.at[b, pl.ds(0, team - 1)]
        pltpu.make_async_copy(arrived, arrived, recv_in.at[b]).wait()
        for a in range(near):
            block = every[b, groups * a : groups * (a + 1)].reshape(groups * local, LANES)
            wide = block.astype(jnp.float32)
            turned = wide.T.astype(jnp.bfloat16)
            rows[b, width * a : width * (a + 1), :F] = turned[:width]
            rows[b, width * a : width * (a + 1), F:] = turned[width:]
            swapped = pltpu.roll(wide, width, 1)
            cols[b, a, :F] = block
            cols[b, a, F:] = jnp.where(first_half, swapped, -swapped).astype(jnp.bfloat16)
        for a in range(near):
            pltpu.make_async_remote_copy(
                src_ref=rows.at[b, pl.ds(width * a, width)],
                dst_ref=rows.at[b, pl.ds(own + width * a, width)],
                send_sem=send_halo,
                recv_sem=recv_halo.at[b * near + a],
                device_id={"chan": behind, "win": win},
                device_id_type=MESH,
            ).start()

    shift = lax.rem(lax.broadcasted_iota(jnp.int32, (1, LANES), 1), width)
    band = BAND // groups
    order = sorted({(step[0], step[2]) for step in steps}, key=lambda s: -hops((s[0], 0, s[1], 0)))

    def multiply(b):
        for a in range(near):
            halo = rows.at[b, pl.ds(own + width * a, width)]
            pltpu.make_async_copy(halo, halo, recv_halo.at[b * near + a]).wait()
            product = jnp.dot(
                rows[b, width * a : width * a + width + BAND],
                cols[b, a],
                preferred_element_type=jnp.float32,
            )
            by = width // 2
            while by >= 8:
                product = jnp.where((shift & by) != 0, product[by:], product[:-by])
                by //= 2
            size = product.shape[0]
            while by >= 1:
                product = jnp.where((shift & by) != 0, pltpu.roll(product, size - by, 0), product)
                by //= 2
            stack[b, a] = product[:BAND].astype(jnp.bfloat16)

            def send_stack(d_hi, d_z, b=b, a=a):
                to_win = win_at(d_hi, d_z)
                pltpu.make_async_remote_copy(
                    src_ref=stack.at[b, a, pl.ds(to_win * band, band)],
                    dst_ref=landing.at[b * team + me],
                    send_sem=send_out,
                    recv_sem=recv_out.at[b],
                    device_id={"chan": base + a, "win": to_win},
                    device_id_type=MESH,
                ).start()

            for d_hi, d_z in order[:-1]:
                send_stack(d_hi, d_z)

            @pl.when(lane_of != a)
            def _(b=b, a=a):
                send_stack(0, 0)

            @pl.when(lane_of == a)
            def _(b=b, a=a):
                landing[b * team + me] = stack[b, a, pl.ds(pl.multiple_of(win * band, band), band)]

    turn(0)
    for b in range(1, bins):
        turn(b)
        multiply(b - 1)
    multiply(bins - 1)

    reach = jnp.concatenate([reach_ref[...], reach_ref[...]], axis=1)
    offset = win * band + lax.broadcasted_iota(jnp.int32, (band, LANES), 0)
    weight_ref[...] = jnp.where(offset < reach, scale, 0.0)
    for b in range(bins):
        pieces = landing.at[pl.ds(b * team, team - 1)]
        pltpu.make_async_copy(pieces, pieces, recv_out.at[b]).wait()
        wide[...] = (
            landing[b * team : (b + 1) * team].astype(jnp.float32).reshape(team * band, LANES)
        )
        for k in range(band):
            out_ref[k, b * team : (b + 1) * team] = wide[pl.ds(k, team, stride=band), :].astype(
                jnp.bfloat16
            )

    sent = mine.at[pl.ds(0, bins * (team - 1))]
    pltpu.make_async_copy(sent, sent, send_in).wait()
    halo = rows.at[pl.ds(0, bins), pl.ds(0, own)]
    pltpu.make_async_copy(halo, halo, send_halo).wait()
    landed = landing.at[pl.ds(0, (team - 1) * bins)]
    pltpu.make_async_copy(landed, landed, send_out).wait()


def exchange(traces, valid, reach, groups, near):
    local, width, samples = traces.shape
    team = near * groups
    bins = F // team
    own = near * width
    band = BAND // groups
    bf16 = jnp.bfloat16
    return pl.pallas_call(
        functools.partial(exchange_kernel, groups, near, 1.0 / math.sqrt(local * groups)),
        out_shape=(pltpu.VMEM((band, F, LANES), bf16), pltpu.VMEM((band, LANES), jnp.float32)),
        in_specs=[pl.BlockSpec(memory_space=pl.ANY)] * 4,
        out_specs=(pl.BlockSpec(memory_space=pltpu.VMEM),) * 2,
        scratch_shapes=[
            pltpu.VMEM((2 * F, samples), bf16),
            pltpu.VMEM((local, width, samples), bf16),
            pltpu.VMEM((local, width), jnp.int32),
            pltpu.VMEM((1, width), jnp.int32),
            pltpu.VMEM((local * F, LANES), jnp.float32),
            pltpu.VMEM((F, local, LANES), bf16),
            pltpu.VMEM((bins, team, local, LANES), bf16),
            pltpu.VMEM((bins, 2 * own, 2 * F), bf16),
            pltpu.VMEM((bins, near, 2 * F, LANES), bf16),
            pltpu.VMEM((bins, near, BAND, LANES), bf16),
            pltpu.VMEM((F, band, LANES), bf16),
            pltpu.VMEM((team * band, LANES), jnp.float32),
            pltpu.SemaphoreType.DMA((4,)),
            pltpu.SemaphoreType.DMA,
            pltpu.SemaphoreType.DMA((bins,)),
            pltpu.SemaphoreType.DMA,
            pltpu.SemaphoreType.DMA((bins * near,)),
            pltpu.SemaphoreType.DMA,
            pltpu.SemaphoreType.DMA((bins,)),
        ],
        compiler_params=pltpu.CompilerParams(collective_id=0, has_side_effects=True),
        name="exchange",
    )(table_rows(samples), traces, valid, reach.reshape(1, width))


def finish_kernel(parts, stack_ref, weight_ref, out_ref, done, sems):
    band, width = out_ref.shape[0], out_ref.shape[1]
    size = band // parts
    copies = []
    for part in range(parts):
        for k in range(part * size, (part + 1) * size):
            turned = (stack_ref[k].astype(jnp.float32) * weight_ref[k : k + 1]).T
            done[k, :, :F] = turned[:width]
            done[k, :, F:] = turned[width:]
        piece = pl.ds(part * size, size)
        copies.append(pltpu.make_async_copy(done.at[piece], out_ref.at[piece], sems.at[part]))
        copies[-1].start()
    for copy in copies:
        copy.wait()


def finish(stacked, weights, width):
    band = stacked.shape[0]
    parts = 8
    stacked = pltpu.with_memory_space_constraint(stacked, pltpu.VMEM)
    weights = pltpu.with_memory_space_constraint(weights, pltpu.VMEM)
    return pl.pallas_call(
        functools.partial(finish_kernel, parts),
        out_shape=jax.ShapeDtypeStruct((band, width, 2 * F), jnp.float32),
        in_specs=[pl.BlockSpec(memory_space=pltpu.VMEM)] * 2,
        out_specs=pl.BlockSpec(memory_space=pl.ANY),
        scratch_shapes=[
            pltpu.VMEM((band, width, 2 * F), jnp.float32),
            pltpu.SemaphoreType.DMA((parts,)),
        ],
        name="finish",
    )(stacked, weights)


def on_device(groups, near, traces, valid, reach):
    stacked, weights = exchange(traces, valid, reach, groups, near)
    return finish(stacked, weights, traces.shape[1])


def solution(mesh):
    groups = mesh.shape["win"]
    near = BAND // (1024 // mesh.shape["chan"])
    in_specs = (P("win", "chan", None), P("win", "chan"), P("chan"))
    return jax.shard_map(
        functools.partial(on_device, groups, near),
        mesh=mesh,
        in_specs=in_specs,
        out_specs=P("win", "chan", None),
        check_vma=False,
    )
```

```python
import functools
import math

import jax
import jax.numpy as jnp
import numpy as np
from jax import lax
from jax.experimental import pallas as pl
from jax.experimental.pallas import tpu as pltpu
from jax.sharding import PartitionSpec as P

F = 128
FIRST = 16
BAND = 256
LANES = 128
MESH = pl.DeviceIdType.MESH


def table_rows(samples):
    t_int = np.arange(samples, dtype=np.int64)
    j_int = np.arange(F, dtype=np.int64) + FIRST
    angle = 2.0 * np.pi / samples * (j_int[:, None] * t_int[None, :] % samples)
    hann = 0.5 - 0.5 * np.cos(2.0 * np.pi / samples * t_int)
    rows = np.concatenate([hann * np.cos(angle), -hann * np.sin(angle)], axis=0)
    return rows.astype(np.float32).astype(jnp.bfloat16)


def exchange_kernel(
    groups, near, scale, table_hbm, traces_hbm, valid_hbm, reach_hbm, out_ref, weight_ref,
    table_ref, traces_ref, valid_ref, reach_ref, spread, mine, every, rows, cols, stack, landing, wide,
    load_sem, send_in, recv_in, send_halo, recv_halo, send_out, recv_out,
):
    chan = lax.axis_index("chan")
    win = lax.axis_index("win")
    ring = lax.axis_size("chan")
    depth = groups // 2
    cores = near // 2
    lane_of = lax.rem(chan, near)
    base = chan - lane_of
    team = near * groups
    bins = F // team
    me = lane_of * groups + win
    width = traces_ref.shape[1]
    local = traces_ref.shape[0]
    ahead = lax.rem(chan + near, ring)
    behind = lax.rem(chan + ring - near, ring)

    y_hi, z = win // depth, lax.rem(win, depth)
    y_lo, core = lane_of // cores, lax.rem(lane_of, cores)

    def hops(step):
        d_hi, d_lo, d_z, d_core = step
        return (1 if d_lo else 2 * d_hi) + min(d_z, depth - d_z)

    steps = [
        (d_hi, d_lo, d_z, d_core)
        for d_hi in range(2)
        for d_lo in range(2)
        for d_z in range(depth)
        for d_core in range(cores)
    ]
    steps.sort(key=lambda step: (-hops(step), step))
    steps.remove((0, 0, 0, 0))

    def win_at(d_hi, d_z):
        return lax.rem(y_hi + d_hi, 2) * depth + lax.rem(z + d_z, depth)

    def lane_at(d_lo, d_core):
        return lax.rem(y_lo + d_lo, 2) * cores + lax.rem(core + d_core, cores)

    loads = [
        pltpu.make_async_copy(table_hbm, table_ref, load_sem.at[0]),
        pltpu.make_async_copy(traces_hbm, traces_ref, load_sem.at[1]),
        pltpu.make_async_copy(valid_hbm, valid_ref, load_sem.at[2]),
        pltpu.make_async_copy(reach_hbm, reach_ref, load_sem.at[3]),
    ]
    for load in loads:
        load.start()

    barrier = pltpu.get_barrier_semaphore()
    for d_hi, d_lo, d_z, d_core in steps:
        pl.semaphore_signal(
            barrier,
            inc=1,
            device_id={"chan": base + lane_at(d_lo, d_core), "win": win_at(d_hi, d_z)},
            device_id_type=MESH,
        )
    for other in (ahead, behind):
        pl.semaphore_signal(
            barrier, inc=1, device_id={"chan": other, "win": win}, device_id_type=MESH
        )

    for load in loads:
        load.wait()

    lane = lax.broadcasted_iota(jnp.int32, (1, LANES), 1)
    first_half = lane < width
    valid_twice = jnp.concatenate([valid_ref[...], valid_ref[...]], axis=1).astype(jnp.float32)
    for pair in range(local // 2):
        samples = traces_ref[2 * pair : 2 * pair + 2].reshape(2 * width, traces_ref.shape[2])
        spectra = lax.dot_general(
            table_ref[...], samples, (((1,), (1,)), ((), ())), preferred_element_type=jnp.float32
        )
        re = spectra[:F]
        im = spectra[F:]
        power = re * re + im * im
        amplitude = jnp.sqrt(power)
        level = jnp.sqrt(jnp.mean(power, axis=0, keepdims=True) + 1e-06)
        usable = jnp.where(
            first_half, valid_twice[2 * pair : 2 * pair + 1], valid_twice[2 * pair + 1 : 2 * pair + 2]
        )
        factor = usable / (amplitude + 0.1 * level)
        re = re * factor
        im = im * factor
        spread[2 * pair * F : 2 * pair * F + F, :] = jnp.where(
            first_half, re, pltpu.roll(im, width, 1)
        )
        spread[(2 * pair + 1) * F : (2 * pair + 1) * F + F, :] = jnp.where(
            first_half, pltpu.roll(re, width, 1), im
        )

    def gather_bin(index, carry):
        mine[index] = spread[pl.ds(index, local, stride=F), :].astype(jnp.bfloat16)
        return carry

    lax.fori_loop(0, F, gather_bin, 0, unroll=8)
    pl.semaphore_wait(barrier, team + 1)

    def send_bins(b, carry):
        for d_hi, d_lo, d_z, d_core in steps:
            to_lane, to_win = lane_at(d_lo, d_core), win_at(d_hi, d_z)
            pltpu.make_async_remote_copy(
                src_ref=mine.at[b * team + to_lane * groups + to_win],
                dst_ref=every.at[b, me],
                send_sem=send_in,
                recv_sem=recv_in.at[b],
                device_id={"chan": base + to_lane, "win": to_win},
                device_id_type=MESH,
            ).start()
        every[b, me] = mine[b * team + me]
        return carry

    lax.fori_loop(0, bins, send_bins, 0)

    own = near * width

    def turn(b):
        arrived = every.at[b, pl.ds(0, team - 1)]
        pltpu.make_async_copy(arrived, arrived, recv_in.at[b]).wait()
        for a in range(near):
            block = every[b, groups * a : groups * (a + 1)].reshape(groups * local, LANES)
            wide = block.astype(jnp.float32)
            turned = wide.T.astype(jnp.bfloat16)
            rows[b, width * a : width * (a + 1), :F] = turned[:width]
            rows[b, width * a : width * (a + 1), F:] = turned[width:]
            swapped = pltpu.roll(wide, width, 1)
            cols[b, a, :F] = block
            cols[b, a, F:] = jnp.where(first_half, swapped, -swapped).astype(jnp.bfloat16)
        for a in range(near):
            pltpu.make_async_remote_copy(
                src_ref=rows.at[b, pl.ds(width * a, width)],
                dst_ref=rows.at[b, pl.ds(own + width * a, width)],
                send_sem=send_halo,
                recv_sem=recv_halo.at[b * near + a],
                device_id={"chan": behind, "win": win},
                device_id_type=MESH,
            ).start()

    shift = lax.rem(lax.broadcasted_iota(jnp.int32, (1, LANES), 1), width)
    band = BAND // groups
    order = sorted({(step[0], step[2]) for step in steps}, key=lambda s: -hops((s[0], 0, s[1], 0)))

    def early(a):
        return max(0, (own - width * a - width) // band)

    def piece(b, a, start, stop):
        first = width * a + band * start
        product = jnp.dot(
            rows[b, first : first + band * (stop - start) + width],
            cols[b, a],
            preferred_element_type=jnp.float32,
        )
        by = width // 2
        while by >= 8:
            product = jnp.where((shift & by) != 0, product[by:], product[:-by])
            by //= 2
        size = product.shape[0]
        while by >= 1:
            product = jnp.where((shift & by) != 0, pltpu.roll(product, size - by, 0), product)
            by //= 2
        stack[b, a, band * start : band * stop] = product[: band * (stop - start)].astype(jnp.bfloat16)

        def send_stack(d_hi, d_z):
            to_win = win_at(d_hi, d_z)

            def send():
                pltpu.make_async_remote_copy(
                    src_ref=stack.at[b, a, pl.ds(to_win * band, band)],
                    dst_ref=landing.at[b * team + me],
                    send_sem=send_out,
                    recv_sem=recv_out.at[b],
                    device_id={"chan": base + a, "win": to_win},
                    device_id_type=MESH,
                ).start()

            if start == 0 and stop == groups:
                send()
            else:
                pl.when((to_win >= start) & (to_win < stop))(send)

        for d_hi, d_z in order[:-1]:
            send_stack(d_hi, d_z)

        @pl.when(lane_of != a)
        def _():
            send_stack(0, 0)

        if stop == groups:

            @pl.when(lane_of == a)
            def _():
                landing[b * team + me] = stack[b, a, pl.ds(pl.multiple_of(win * band, band), band)]

    def multiply_early(b):
        for a in range(near):
            if early(a):
                piece(b, a, 0, early(a))

    def multiply(b):
        for a in range(near):
            halo = rows.at[b, pl.ds(own + width * a, width)]
            pltpu.make_async_copy(halo, halo, recv_halo.at[b * near + a]).wait()
            piece(b, a, early(a), groups)

    for b in range(bins):
        turn(b)
        multiply_early(b)
        if b > 0:
            multiply(b - 1)
    multiply(bins - 1)

    reach = jnp.concatenate([reach_ref[...], reach_ref[...]], axis=1)
    offset = win * band + lax.broadcasted_iota(jnp.int32, (band, LANES), 0)
    weight_ref[...] = jnp.where(offset < reach, scale, 0.0)
    for b in range(bins):
        pieces = landing.at[pl.ds(b * team, team - 1)]
        pltpu.make_async_copy(pieces, pieces, recv_out.at[b]).wait()
        wide[...] = (
            landing[b * team : (b + 1) * team].astype(jnp.float32).reshape(team * band, LANES)
        )
        for k in range(band):
            out_ref[k, b * team : (b + 1) * team] = wide[pl.ds(k, team, stride=band), :].astype(
                jnp.bfloat16
            )

    sent = mine.at[pl.ds(0, bins * (team - 1))]
    pltpu.make_async_copy(sent, sent, send_in).wait()
    halo = rows.at[pl.ds(0, bins), pl.ds(0, own)]
    pltpu.make_async_copy(halo, halo, send_halo).wait()
    landed = landing.at[pl.ds(0, (team - 1) * bins)]
    pltpu.make_async_copy(landed, landed, send_out).wait()


def exchange(traces, valid, reach, groups, near):
    local, width, samples = traces.shape
    team = near * groups
    bins = F // team
    own = near * width
    band = BAND // groups
    bf16 = jnp.bfloat16
    return pl.pallas_call(
        functools.partial(exchange_kernel, groups, near, 1.0 / math.sqrt(local * groups)),
        out_shape=(pltpu.VMEM((band, F, LANES), bf16), pltpu.VMEM((band, LANES), jnp.float32)),
        in_specs=[pl.BlockSpec(memory_space=pl.ANY)] * 4,
        out_specs=(pl.BlockSpec(memory_space=pltpu.VMEM),) * 2,
        scratch_shapes=[
            pltpu.VMEM((2 * F, samples), bf16),
            pltpu.VMEM((local, width, samples), bf16),
            pltpu.VMEM((local, width), jnp.int32),
            pltpu.VMEM((1, width), jnp.int32),
            pltpu.VMEM((local * F, LANES), jnp.float32),
            pltpu.VMEM((F, local, LANES), bf16),
            pltpu.VMEM((bins, team, local, LANES), bf16),
            pltpu.VMEM((bins, 2 * own, 2 * F), bf16),
            pltpu.VMEM((bins, near, 2 * F, LANES), bf16),
            pltpu.VMEM((bins, near, BAND, LANES), bf16),
            pltpu.VMEM((F, band, LANES), bf16),
            pltpu.VMEM((team * band, LANES), jnp.float32),
            pltpu.SemaphoreType.DMA((4,)),
            pltpu.SemaphoreType.DMA,
            pltpu.SemaphoreType.DMA((bins,)),
            pltpu.SemaphoreType.DMA,
            pltpu.SemaphoreType.DMA((bins * near,)),
            pltpu.SemaphoreType.DMA,
            pltpu.SemaphoreType.DMA((bins,)),
        ],
        compiler_params=pltpu.CompilerParams(collective_id=0, has_side_effects=True),
        name="exchange",
    )(table_rows(samples), traces, valid, reach.reshape(1, width))


def finish_kernel(parts, stack_ref, weight_ref, out_ref, done, sems):
    band, width = out_ref.shape[0], out_ref.shape[1]
    size = band // parts
    copies = []
    for part in range(parts):
        for k in range(part * size, (part + 1) * size):
            turned = (stack_ref[k].astype(jnp.float32) * weight_ref[k : k + 1]).T
            done[k, :, :F] = turned[:width]
            done[k, :, F:] = turned[width:]
        piece = pl.ds(part * size, size)
        copies.append(pltpu.make_async_copy(done.at[piece], out_ref.at[piece], sems.at[part]))
        copies[-1].start()
    for copy in copies:
        copy.wait()


def finish(stacked, weights, width):
    band = stacked.shape[0]
    parts = 8
    stacked = pltpu.with_memory_space_constraint(stacked, pltpu.VMEM)
    weights = pltpu.with_memory_space_constraint(weights, pltpu.VMEM)
    return pl.pallas_call(
        functools.partial(finish_kernel, parts),
        out_shape=jax.ShapeDtypeStruct((band, width, 2 * F), jnp.float32),
        in_specs=[pl.BlockSpec(memory_space=pltpu.VMEM)] * 2,
        out_specs=pl.BlockSpec(memory_space=pl.ANY),
        scratch_shapes=[
            pltpu.VMEM((band, width, 2 * F), jnp.float32),
            pltpu.SemaphoreType.DMA((parts,)),
        ],
        name="finish",
    )(stacked, weights)


def on_device(groups, near, traces, valid, reach):
    stacked, weights = exchange(traces, valid, reach, groups, near)
    return finish(stacked, weights, traces.shape[1])


def solution(mesh):
    groups = mesh.shape["win"]
    near = BAND // (1024 // mesh.shape["chan"])
    in_specs = (P("win", "chan", None), P("win", "chan"), P("chan"))
    return jax.shard_map(
        functools.partial(on_device, groups, near),
        mesh=mesh,
        in_specs=in_specs,
        out_specs=P("win", "chan", None),
        check_vma=False,
    )
```

```python
import functools
import math

import jax
import jax.numpy as jnp
import numpy as np
from jax import lax
from jax.experimental import pallas as pl
from jax.experimental.pallas import tpu as pltpu
from jax.sharding import PartitionSpec as P

F = 128
FIRST = 16
BAND = 256
LANES = 128
MESH = pl.DeviceIdType.MESH


def table_rows(samples):
    t_int = np.arange(samples, dtype=np.int64)
    j_int = np.arange(F, dtype=np.int64) + FIRST
    angle = 2.0 * np.pi / samples * (j_int[:, None] * t_int[None, :] % samples)
    hann = 0.5 - 0.5 * np.cos(2.0 * np.pi / samples * t_int)
    rows = np.concatenate([hann * np.cos(angle), -hann * np.sin(angle)], axis=0)
    return rows.astype(np.float32).astype(jnp.bfloat16)


def exchange_kernel(
    groups, near, scale, table_hbm, traces_hbm, valid_hbm, reach_hbm, out_ref, weight_ref,
    table_ref, traces_ref, valid_ref, reach_ref, spread, mine, every, rows, cols, stack, landing, wide,
    load_sem, send_in, recv_in, send_halo, recv_halo, send_out, recv_out,
):
    chan = lax.axis_index("chan")
    win = lax.axis_index("win")
    ring = lax.axis_size("chan")
    depth = groups // 2
    cores = near // 2
    lane_of = lax.rem(chan, near)
    base = chan - lane_of
    team = near * groups
    bins = F // team
    me = lane_of * groups + win
    width = traces_ref.shape[1]
    local = traces_ref.shape[0]
    ahead = lax.rem(chan + near, ring)
    behind = lax.rem(chan + ring - near, ring)

    y_hi, z = win // depth, lax.rem(win, depth)
    y_lo, core = lane_of // cores, lax.rem(lane_of, cores)

    def hops(step):
        d_hi, d_lo, d_z, d_core = step
        return (1 if d_lo else 2 * d_hi) + min(d_z, depth - d_z)

    steps = [
        (d_hi, d_lo, d_z, d_core)
        for d_hi in range(2)
        for d_lo in range(2)
        for d_z in range(depth)
        for d_core in range(cores)
    ]
    steps.sort(key=lambda step: (-hops(step), step))
    steps.remove((0, 0, 0, 0))

    def win_at(d_hi, d_z):
        return lax.rem(y_hi + d_hi, 2) * depth + lax.rem(z + d_z, depth)

    def lane_at(d_lo, d_core):
        return lax.rem(y_lo + d_lo, 2) * cores + lax.rem(core + d_core, cores)

    loads = [
        pltpu.make_async_copy(table_hbm, table_ref, load_sem.at[0]),
        pltpu.make_async_copy(traces_hbm, traces_ref, load_sem.at[1]),
        pltpu.make_async_copy(valid_hbm, valid_ref, load_sem.at[2]),
        pltpu.make_async_copy(reach_hbm, reach_ref, load_sem.at[3]),
    ]
    for load in loads:
        load.start()

    barrier = pltpu.get_barrier_semaphore()
    for d_hi, d_lo, d_z, d_core in steps:
        pl.semaphore_signal(
            barrier,
            inc=1,
            device_id={"chan": base + lane_at(d_lo, d_core), "win": win_at(d_hi, d_z)},
            device_id_type=MESH,
        )
    for other in (ahead, behind):
        pl.semaphore_signal(
            barrier, inc=1, device_id={"chan": other, "win": win}, device_id_type=MESH
        )

    for load in loads:
        load.wait()

    lane = lax.broadcasted_iota(jnp.int32, (1, LANES), 1)
    first_half = lane < width
    valid_twice = jnp.concatenate([valid_ref[...], valid_ref[...]], axis=1).astype(jnp.float32)
    for pair in range(local // 2):
        samples = traces_ref[2 * pair : 2 * pair + 2].reshape(2 * width, traces_ref.shape[2])
        spectra = lax.dot_general(
            table_ref[...], samples, (((1,), (1,)), ((), ())), preferred_element_type=jnp.float32
        )
        re = spectra[:F]
        im = spectra[F:]
        power = re * re + im * im
        amplitude = jnp.sqrt(power)
        level = jnp.sqrt(jnp.mean(power, axis=0, keepdims=True) + 1e-06)
        usable = jnp.where(
            first_half, valid_twice[2 * pair : 2 * pair + 1], valid_twice[2 * pair + 1 : 2 * pair + 2]
        )
        factor = usable / (amplitude + 0.1 * level)
        re = re * factor
        im = im * factor
        spread[2 * pair * F : 2 * pair * F + F, :] = jnp.where(
            first_half, re, pltpu.roll(im, width, 1)
        )
        spread[(2 * pair + 1) * F : (2 * pair + 1) * F + F, :] = jnp.where(
            first_half, pltpu.roll(re, width, 1), im
        )

    def gather_bin(index, carry):
        mine[index] = spread[pl.ds(index, local, stride=F), :].astype(jnp.bfloat16)
        return carry

    lax.fori_loop(0, F, gather_bin, 0, unroll=8)
    pl.semaphore_wait(barrier, team + 1)

    def send_bins(b, carry):
        for d_hi, d_lo, d_z, d_core in steps:
            to_lane, to_win = lane_at(d_lo, d_core), win_at(d_hi, d_z)
            pltpu.make_async_remote_copy(
                src_ref=mine.at[b * team + to_lane * groups + to_win],
                dst_ref=every.at[b, me],
                send_sem=send_in,
                recv_sem=recv_in.at[b],
                device_id={"chan": base + to_lane, "win": to_win},
                device_id_type=MESH,
            ).start()
        every[b, me] = mine[b * team + me]
        return carry

    lax.fori_loop(0, bins, send_bins, 0)

    own = near * width

    def turn(b):
        arrived = every.at[b, pl.ds(0, team - 1)]
        pltpu.make_async_copy(arrived, arrived, recv_in.at[b]).wait()
        for a in range(near):
            block = every[b, groups * a : groups * (a + 1)].reshape(groups * local, LANES)
            wide = block.astype(jnp.float32)
            turned = wide.T.astype(jnp.bfloat16)
            rows[b, width * a : width * (a + 1), :F] = turned[:width]
            rows[b, width * a : width * (a + 1), F:] = turned[width:]
            swapped = pltpu.roll(wide, width, 1)
            cols[b, a, :F] = block
            cols[b, a, F:] = jnp.where(first_half, swapped, -swapped).astype(jnp.bfloat16)
        for a in range(near):
            pltpu.make_async_remote_copy(
                src_ref=rows.at[b, pl.ds(width * a, width)],
                dst_ref=rows.at[b, pl.ds(own + width * a, width)],
                send_sem=send_halo,
                recv_sem=recv_halo.at[b * near + a],
                device_id={"chan": behind, "win": win},
                device_id_type=MESH,
            ).start()

    shift = lax.rem(lax.broadcasted_iota(jnp.int32, (1, LANES), 1), width)
    band = BAND // groups
    order = sorted(sorted({(step[0], step[2]) for step in steps}), key=lambda s: -hops((s[0], 0, s[1], 0)))

    def early(a):
        return max(0, (own - width * a - width) // band)

    def piece(b, a, start, stop):
        first = width * a + band * start
        product = jnp.dot(
            rows[b, first : first + band * (stop - start) + width],
            cols[b, a],
            preferred_element_type=jnp.float32,
        )
        by = width // 2
        while by >= 8:
            product = jnp.where((shift & by) != 0, product[by:], product[:-by])
            by //= 2
        size = product.shape[0]
        while by >= 1:
            product = jnp.where((shift & by) != 0, pltpu.roll(product, size - by, 0), product)
            by //= 2
        stack[b, a, band * start : band * stop] = product[: band * (stop - start)].astype(jnp.bfloat16)

        def send_stack(to_win):
            pltpu.make_async_remote_copy(
                src_ref=stack.at[b, a, pl.ds(to_win * band, band)],
                dst_ref=landing.at[b * team + me],
                send_sem=send_out,
                recv_sem=recv_out.at[b],
                device_id={"chan": base + a, "win": to_win},
                device_id_type=MESH,
            ).start()

        if stop - start <= width // band:
            for to_win in range(start, stop):
                pl.when((lane_of != a) | (win != to_win))(functools.partial(send_stack, to_win))
        else:
            for d_hi, d_z in order:
                to_win = win_at(d_hi, d_z)
                wanted = (to_win >= start) & (to_win < stop)
                if (d_hi, d_z) == (0, 0):
                    wanted = wanted & (lane_of != a)
                pl.when(wanted)(functools.partial(send_stack, to_win))

        @pl.when((lane_of == a) & (win >= start) & (win < stop))
        def _():
            landing[b * team + me] = stack[b, a, pl.ds(pl.multiple_of(win * band, band), band)]

    def multiply_early(b):
        for a in range(near):
            if early(a):
                piece(b, a, 0, early(a))

    def multiply(b):
        step = width // band
        for h in range(near):
            halo = rows.at[b, pl.ds(own + width * h, width)]
            pltpu.make_async_copy(halo, halo, recv_halo.at[b * near + h]).wait()
            for a in range(near - 1, h - 1, -1):
                start = step * (near - 1 - a + h)
                piece(b, a, start, start + step)

    for b in range(bins):
        turn(b)
        multiply_early(b)
        if b > 0:
            multiply(b - 1)
    multiply(bins - 1)

    reach = jnp.concatenate([reach_ref[...], reach_ref[...]], axis=1)
    offset = win * band + lax.broadcasted_iota(jnp.int32, (band, LANES), 0)
    weight_ref[...] = jnp.where(offset < reach, scale, 0.0)
    for b in range(bins):
        pieces = landing.at[pl.ds(b * team, team - 1)]
        pltpu.make_async_copy(pieces, pieces, recv_out.at[b]).wait()
        wide[...] = (
            landing[b * team : (b + 1) * team].astype(jnp.float32).reshape(team * band, LANES)
        )
        for k in range(band):
            out_ref[k, b * team : (b + 1) * team] = wide[pl.ds(k, team, stride=band), :].astype(
                jnp.bfloat16
            )

    sent = mine.at[pl.ds(0, bins * (team - 1))]
    pltpu.make_async_copy(sent, sent, send_in).wait()
    halo = rows.at[pl.ds(0, bins), pl.ds(0, own)]
    pltpu.make_async_copy(halo, halo, send_halo).wait()
    landed = landing.at[pl.ds(0, (team - 1) * bins)]
    pltpu.make_async_copy(landed, landed, send_out).wait()


def exchange(traces, valid, reach, groups, near):
    local, width, samples = traces.shape
    team = near * groups
    bins = F // team
    own = near * width
    band = BAND // groups
    bf16 = jnp.bfloat16
    return pl.pallas_call(
        functools.partial(exchange_kernel, groups, near, 1.0 / math.sqrt(local * groups)),
        out_shape=(pltpu.VMEM((band, F, LANES), bf16), pltpu.VMEM((band, LANES), jnp.float32)),
        in_specs=[pl.BlockSpec(memory_space=pl.ANY)] * 4,
        out_specs=(pl.BlockSpec(memory_space=pltpu.VMEM),) * 2,
        scratch_shapes=[
            pltpu.VMEM((2 * F, samples), bf16),
            pltpu.VMEM((local, width, samples), bf16),
            pltpu.VMEM((local, width), jnp.int32),
            pltpu.VMEM((1, width), jnp.int32),
            pltpu.VMEM((local * F, LANES), jnp.float32),
            pltpu.VMEM((F, local, LANES), bf16),
            pltpu.VMEM((bins, team, local, LANES), bf16),
            pltpu.VMEM((bins, 2 * own, 2 * F), bf16),
            pltpu.VMEM((bins, near, 2 * F, LANES), bf16),
            pltpu.VMEM((bins, near, BAND, LANES), bf16),
            pltpu.VMEM((F, band, LANES), bf16),
            pltpu.VMEM((team * band, LANES), jnp.float32),
            pltpu.SemaphoreType.DMA((4,)),
            pltpu.SemaphoreType.DMA,
            pltpu.SemaphoreType.DMA((bins,)),
            pltpu.SemaphoreType.DMA,
            pltpu.SemaphoreType.DMA((bins * near,)),
            pltpu.SemaphoreType.DMA,
            pltpu.SemaphoreType.DMA((bins,)),
        ],
        compiler_params=pltpu.CompilerParams(collective_id=0, has_side_effects=True),
        name="exchange",
    )(table_rows(samples), traces, valid, reach.reshape(1, width))


def finish_kernel(parts, stack_ref, weight_ref, out_ref, done, sems):
    band, width = out_ref.shape[0], out_ref.shape[1]
    size = band // parts
    copies = []
    for part in range(parts):
        for k in range(part * size, (part + 1) * size):
            turned = (stack_ref[k].astype(jnp.float32) * weight_ref[k : k + 1]).T
            done[k, :, :F] = turned[:width]
            done[k, :, F:] = turned[width:]
        piece = pl.ds(part * size, size)
        copies.append(pltpu.make_async_copy(done.at[piece], out_ref.at[piece], sems.at[part]))
        copies[-1].start()
    for copy in copies:
        copy.wait()


def finish(stacked, weights, width):
    band = stacked.shape[0]
    parts = 8
    stacked = pltpu.with_memory_space_constraint(stacked, pltpu.VMEM)
    weights = pltpu.with_memory_space_constraint(weights, pltpu.VMEM)
    return pl.pallas_call(
        functools.partial(finish_kernel, parts),
        out_shape=jax.ShapeDtypeStruct((band, width, 2 * F), jnp.float32),
        in_specs=[pl.BlockSpec(memory_space=pltpu.VMEM)] * 2,
        out_specs=pl.BlockSpec(memory_space=pl.ANY),
        scratch_shapes=[
            pltpu.VMEM((band, width, 2 * F), jnp.float32),
            pltpu.SemaphoreType.DMA((parts,)),
        ],
        name="finish",
    )(stacked, weights)


def on_device(groups, near, traces, valid, reach):
    stacked, weights = exchange(traces, valid, reach, groups, near)
    return finish(stacked, weights, traces.shape[1])


def solution(mesh):
    groups = mesh.shape["win"]
    near = BAND // (1024 // mesh.shape["chan"])
    in_specs = (P("win", "chan", None), P("win", "chan"), P("chan"))
    return jax.shard_map(
        functools.partial(on_device, groups, near),
        mesh=mesh,
        in_specs=in_specs,
        out_specs=P("win", "chan", None),
        check_vma=False,
    )
```

```python
import functools
import math

import jax
import jax.numpy as jnp
import numpy as np
from jax import lax
from jax.experimental import pallas as pl
from jax.experimental.pallas import tpu as pltpu
from jax.sharding import PartitionSpec as P

F = 128
FIRST = 16
BAND = 256
LANES = 128
MESH = pl.DeviceIdType.MESH


def table_rows(samples):
    t_int = np.arange(samples, dtype=np.int64)
    j_int = np.arange(F, dtype=np.int64) + FIRST
    angle = 2.0 * np.pi / samples * (j_int[:, None] * t_int[None, :] % samples)
    hann = 0.5 - 0.5 * np.cos(2.0 * np.pi / samples * t_int)
    rows = np.concatenate([hann * np.cos(angle), -hann * np.sin(angle)], axis=0)
    return rows.astype(np.float32).astype(jnp.bfloat16)


def exchange_kernel(
    groups, near, scale, table_hbm, traces_hbm, valid_hbm, reach_hbm, out_ref, weight_ref,
    table_ref, traces_ref, valid_ref, reach_ref, spread, mine, every, rows, cols, stack, landing, wide,
    load_sem, send_in, recv_in, send_halo, recv_halo, send_out, recv_out,
):
    chan = lax.axis_index("chan")
    win = lax.axis_index("win")
    ring = lax.axis_size("chan")
    depth = groups // 2
    cores = near // 2
    lane_of = lax.rem(chan, near)
    base = chan - lane_of
    team = near * groups
    bins = F // team
    me = lane_of * groups + win
    width = traces_ref.shape[1]
    local = traces_ref.shape[0]
    ahead = lax.rem(chan + near, ring)
    behind = lax.rem(chan + ring - near, ring)

    y_hi, z = win // depth, lax.rem(win, depth)
    y_lo, core = lane_of // cores, lax.rem(lane_of, cores)

    def hops(step):
        d_hi, d_lo, d_z, d_core = step
        return (1 if d_lo else 2 * d_hi) + min(d_z, depth - d_z)

    steps = [
        (d_hi, d_lo, d_z, d_core)
        for d_hi in range(2)
        for d_lo in range(2)
        for d_z in range(depth)
        for d_core in range(cores)
    ]
    steps.sort(key=lambda step: (-hops(step), step))
    steps.remove((0, 0, 0, 0))

    def win_at(d_hi, d_z):
        return lax.rem(y_hi + d_hi, 2) * depth + lax.rem(z + d_z, depth)

    def lane_at(d_lo, d_core):
        return lax.rem(y_lo + d_lo, 2) * cores + lax.rem(core + d_core, cores)

    loads = [
        pltpu.make_async_copy(table_hbm, table_ref, load_sem.at[0]),
        pltpu.make_async_copy(traces_hbm, traces_ref, load_sem.at[1]),
        pltpu.make_async_copy(valid_hbm, valid_ref, load_sem.at[2]),
        pltpu.make_async_copy(reach_hbm, reach_ref, load_sem.at[3]),
    ]
    for load in loads:
        load.start()

    barrier = pltpu.get_barrier_semaphore()
    for d_hi, d_lo, d_z, d_core in steps:
        pl.semaphore_signal(
            barrier,
            inc=1,
            device_id={"chan": base + lane_at(d_lo, d_core), "win": win_at(d_hi, d_z)},
            device_id_type=MESH,
        )
    for other in (ahead, behind):
        pl.semaphore_signal(
            barrier, inc=1, device_id={"chan": other, "win": win}, device_id_type=MESH
        )

    for load in loads:
        load.wait()

    lane = lax.broadcasted_iota(jnp.int32, (1, LANES), 1)
    first_half = lane < width
    valid_twice = jnp.concatenate([valid_ref[...], valid_ref[...]], axis=1).astype(jnp.float32)
    for pair in range(local // 2):
        samples = traces_ref[2 * pair : 2 * pair + 2].reshape(2 * width, traces_ref.shape[2])
        spectra = lax.dot_general(
            table_ref[...], samples, (((1,), (1,)), ((), ())), preferred_element_type=jnp.float32
        )
        re = spectra[:F]
        im = spectra[F:]
        power = re * re + im * im
        amplitude = jnp.sqrt(power)
        level = jnp.sqrt(jnp.mean(power, axis=0, keepdims=True) + 1e-06)
        usable = jnp.where(
            first_half, valid_twice[2 * pair : 2 * pair + 1], valid_twice[2 * pair + 1 : 2 * pair + 2]
        )
        factor = usable / (amplitude + 0.1 * level)
        re = re * factor
        im = im * factor
        spread[2 * pair * F : 2 * pair * F + F, :] = jnp.where(
            first_half, re, pltpu.roll(im, width, 1)
        )
        spread[(2 * pair + 1) * F : (2 * pair + 1) * F + F, :] = jnp.where(
            first_half, pltpu.roll(re, width, 1), im
        )

    def gather_bin(index, carry):
        mine[index] = spread[pl.ds(index, local, stride=F), :].astype(jnp.bfloat16)
        return carry

    lax.fori_loop(0, F, gather_bin, 0, unroll=8)
    pl.semaphore_wait(barrier, team + 1)

    def send_bins(b, carry):
        for d_hi, d_lo, d_z, d_core in steps:
            to_lane, to_win = lane_at(d_lo, d_core), win_at(d_hi, d_z)
            pltpu.make_async_remote_copy(
                src_ref=mine.at[b * team + to_lane * groups + to_win],
                dst_ref=every.at[b, me],
                send_sem=send_in,
                recv_sem=recv_in.at[b],
                device_id={"chan": base + to_lane, "win": to_win},
                device_id_type=MESH,
            ).start()
        every[b, me] = mine[b * team + me]
        return carry

    lax.fori_loop(0, bins, send_bins, 0)

    own = near * width

    def turn(b):
        arrived = every.at[b, pl.ds(0, team - 1)]
        pltpu.make_async_copy(arrived, arrived, recv_in.at[b]).wait()
        for a in range(near):
            block = every[b, groups * a : groups * (a + 1)].reshape(groups * local, LANES)
            wide = block.astype(jnp.float32)
            turned = wide.T.astype(jnp.bfloat16)
            rows[b, width * a : width * (a + 1), :F] = turned[:width]
            rows[b, width * a : width * (a + 1), F:] = turned[width:]
            swapped = pltpu.roll(wide, width, 1)
            cols[b, a, :F] = block
            cols[b, a, F:] = jnp.where(first_half, swapped, -swapped).astype(jnp.bfloat16)
        for a in range(near):
            pltpu.make_async_remote_copy(
                src_ref=rows.at[b, pl.ds(width * a, width)],
                dst_ref=rows.at[b, pl.ds(own + width * a, width)],
                send_sem=send_halo,
                recv_sem=recv_halo.at[b * near + a],
                device_id={"chan": behind, "win": win},
                device_id_type=MESH,
            ).start()

    shift = lax.rem(lax.broadcasted_iota(jnp.int32, (1, LANES), 1), width)
    band = BAND // groups
    order = sorted(sorted({(step[0], step[2]) for step in steps}), key=lambda s: -hops((s[0], 0, s[1], 0)))

    def early(a):
        return max(0, (own - width * a - width) // band)

    def piece(b, a, start, stop):
        first = width * a + band * start
        product = jnp.dot(
            rows[b, first : first + band * (stop - start) + width],
            cols[b, a],
            preferred_element_type=jnp.float32,
        )
        by = width // 2
        while by >= 8:
            product = jnp.where((shift & by) != 0, product[by:], product[:-by])
            by //= 2
        size = product.shape[0]
        while by >= 1:
            product = jnp.where((shift & by) != 0, pltpu.roll(product, size - by, 0), product)
            by //= 2
        stack[b, a, band * start : band * stop] = product[: band * (stop - start)].astype(jnp.bfloat16)

    def dispatch(b, a, start, stop):
        def send_stack(to_win):
            pltpu.make_async_remote_copy(
                src_ref=stack.at[b, a, pl.ds(to_win * band, band)],
                dst_ref=landing.at[b * team + me],
                send_sem=send_out,
                recv_sem=recv_out.at[b],
                device_id={"chan": base + a, "win": to_win},
                device_id_type=MESH,
            ).start()

        if stop - start <= width // band:
            for to_win in range(start, stop):
                pl.when((lane_of != a) | (win != to_win))(functools.partial(send_stack, to_win))
        else:
            for d_hi, d_z in order:
                to_win = win_at(d_hi, d_z)
                wanted = (to_win >= start) & (to_win < stop)
                if (d_hi, d_z) == (0, 0):
                    wanted = wanted & (lane_of != a)
                pl.when(wanted)(functools.partial(send_stack, to_win))

        @pl.when((lane_of == a) & (win >= start) & (win < stop))
        def _():
            landing[b * team + me] = stack[b, a, pl.ds(pl.multiple_of(win * band, band), band)]

    def pieces(b, parts):
        for part in parts:
            piece(b, *part)
        for part in parts:
            dispatch(b, *part)

    def multiply_early(b):
        pieces(b, [(a, 0, early(a)) for a in range(near) if early(a)])

    def multiply(b):
        step = width // band
        for h in range(near):
            halo = rows.at[b, pl.ds(own + width * h, width)]
            pltpu.make_async_copy(halo, halo, recv_halo.at[b * near + h]).wait()
            starts = [(a, step * (near - 1 - a + h)) for a in range(near - 1, h - 1, -1)]
            pieces(b, [(a, start, start + step) for a, start in starts])

    for b in range(bins):
        turn(b)
        multiply_early(b)
        if b > 1:
            multiply(b - 2)
    multiply(bins - 2)
    multiply(bins - 1)

    reach = jnp.concatenate([reach_ref[...], reach_ref[...]], axis=1)
    offset = win * band + lax.broadcasted_iota(jnp.int32, (band, LANES), 0)
    weight_ref[...] = jnp.where(offset < reach, scale, 0.0)
    for b in range(bins):
        pieces = landing.at[pl.ds(b * team, team - 1)]
        pltpu.make_async_copy(pieces, pieces, recv_out.at[b]).wait()
        wide[...] = (
            landing[b * team : (b + 1) * team].astype(jnp.float32).reshape(team * band, LANES)
        )
        for k in range(band):
            out_ref[k, b * team : (b + 1) * team] = wide[pl.ds(k, team, stride=band), :].astype(
                jnp.bfloat16
            )

    sent = mine.at[pl.ds(0, bins * (team - 1))]
    pltpu.make_async_copy(sent, sent, send_in).wait()
    halo = rows.at[pl.ds(0, bins), pl.ds(0, own)]
    pltpu.make_async_copy(halo, halo, send_halo).wait()
    landed = landing.at[pl.ds(0, (team - 1) * bins)]
    pltpu.make_async_copy(landed, landed, send_out).wait()


def exchange(traces, valid, reach, groups, near):
    local, width, samples = traces.shape
    team = near * groups
    bins = F // team
    own = near * width
    band = BAND // groups
    bf16 = jnp.bfloat16
    return pl.pallas_call(
        functools.partial(exchange_kernel, groups, near, 1.0 / math.sqrt(local * groups)),
        out_shape=(pltpu.VMEM((band, F, LANES), bf16), pltpu.VMEM((band, LANES), jnp.float32)),
        in_specs=[pl.BlockSpec(memory_space=pl.ANY)] * 4,
        out_specs=(pl.BlockSpec(memory_space=pltpu.VMEM),) * 2,
        scratch_shapes=[
            pltpu.VMEM((2 * F, samples), bf16),
            pltpu.VMEM((local, width, samples), bf16),
            pltpu.VMEM((local, width), jnp.int32),
            pltpu.VMEM((1, width), jnp.int32),
            pltpu.VMEM((local * F, LANES), jnp.float32),
            pltpu.VMEM((F, local, LANES), bf16),
            pltpu.VMEM((bins, team, local, LANES), bf16),
            pltpu.VMEM((bins, 2 * own, 2 * F), bf16),
            pltpu.VMEM((bins, near, 2 * F, LANES), bf16),
            pltpu.VMEM((bins, near, BAND, LANES), bf16),
            pltpu.VMEM((F, band, LANES), bf16),
            pltpu.VMEM((team * band, LANES), jnp.float32),
            pltpu.SemaphoreType.DMA((4,)),
            pltpu.SemaphoreType.DMA,
            pltpu.SemaphoreType.DMA((bins,)),
            pltpu.SemaphoreType.DMA,
            pltpu.SemaphoreType.DMA((bins * near,)),
            pltpu.SemaphoreType.DMA,
            pltpu.SemaphoreType.DMA((bins,)),
        ],
        compiler_params=pltpu.CompilerParams(collective_id=0, has_side_effects=True),
        name="exchange",
    )(table_rows(samples), traces, valid, reach.reshape(1, width))


def finish_kernel(parts, stack_ref, weight_ref, out_ref, done, sems):
    band, width = out_ref.shape[0], out_ref.shape[1]
    size = band // parts
    copies = []
    for part in range(parts):
        for k in range(part * size, (part + 1) * size):
            turned = (stack_ref[k].astype(jnp.float32) * weight_ref[k : k + 1]).T
            done[k, :, :F] = turned[:width]
            done[k, :, F:] = turned[width:]
        piece = pl.ds(part * size, size)
        copies.append(pltpu.make_async_copy(done.at[piece], out_ref.at[piece], sems.at[part]))
        copies[-1].start()
    for copy in copies:
        copy.wait()


def finish(stacked, weights, width):
    band = stacked.shape[0]
    parts = 4
    stacked = pltpu.with_memory_space_constraint(stacked, pltpu.VMEM)
    weights = pltpu.with_memory_space_constraint(weights, pltpu.VMEM)
    return pl.pallas_call(
        functools.partial(finish_kernel, parts),
        out_shape=jax.ShapeDtypeStruct((band, width, 2 * F), jnp.float32),
        in_specs=[pl.BlockSpec(memory_space=pltpu.VMEM)] * 2,
        out_specs=pl.BlockSpec(memory_space=pl.ANY),
        scratch_shapes=[
            pltpu.VMEM((band, width, 2 * F), jnp.float32),
            pltpu.SemaphoreType.DMA((parts,)),
        ],
        name="finish",
    )(stacked, weights)


def on_device(groups, near, traces, valid, reach):
    stacked, weights = exchange(traces, valid, reach, groups, near)
    return finish(stacked, weights, traces.shape[1])


def solution(mesh):
    groups = mesh.shape["win"]
    near = BAND // (1024 // mesh.shape["chan"])
    in_specs = (P("win", "chan", None), P("win", "chan"), P("chan"))
    return jax.shard_map(
        functools.partial(on_device, groups, near),
        mesh=mesh,
        in_specs=in_specs,
        out_specs=P("win", "chan", None),
        check_vma=False,
    )
```
